512 devices in a mesh: row: 32 (over x, z), col: 16 (over y, core).
Axes of the slice: x: 4, y: 8, z: 8, core: 2. Of those that a mesh axis runs over, the one named last changes fastest.
Arguments:
- rhs_top: float32 [2, 32768, 2048], P(None, 'row', 'col'), may hold values from -6 to 6
- rhs_low: float32 [2, 2, 512, 2048], P(None, None, 'row', 'col'), may hold values from -6 to 6
- inv_diag: float32 [2, 2, 512, 512], P(None, None, 'row'), may hold values from -3 to 3, as said below
- coupling: float32 [2, 512, 512], P(None, 'row'), may hold values from -0.1875 to 0.1875
- panel: float32 [2, 32768, 1024], P(None, 'row', 'col'), may hold values from -0.125 to 0.125
- radiation: float32 [2, 4096, 1024], P(None, 'row'), may hold values from -0.125 to 0.125
Outputs:
- solved: float32 [2, 2, 512, 2048], P(None, None, 'row', 'col')
- updated_top: float32 [2, 32768, 2048], P(None, 'row', 'col')
- far_field: float32 [2, 4096, 2048], P(None, 'row', 'col')
The draws below stay inside these ranges and needn't reach their ends.
Inputs may be any that keep to these rules, and one draw needn't show every extreme that they name: `inv_diag`: each of the two 512 x 512 complex blocks is upper triangular.
All inputs are finite; a program needn't handle non-finite values.
Results may differ from the reference program's by a relative error of at most 0.000094.
Values sent between devices are 32-bit elements; how exact they have to be, the bound alone decides.
No kernel may reach another device: no remote copies, remote signals or barrier semaphores. Data moves between devices by JAX's collectives and lax.ppermute only.
A program may use at most 64 MiB of HBM per device.

```python
import math
import jax
import jax.numpy as jnp
from jax import lax

NB = 512
DIRS = 2048
ANG = 2048
ABOVE = 32768


def draw_inv_diag(key, part):
    noise_key, real_key, imag_key = jax.random.split(key, 3)
    noise = jax.random.normal(noise_key, (2, 2, NB, NB), jnp.float32)
    upper = jnp.triu(noise * (0.7 / math.sqrt(NB)), 1)
    diag_real = jax.random.uniform(real_key, (2, NB), jnp.float32, 0.7, 1.4)
    diag_imag = jax.random.uniform(imag_key, (2, NB), jnp.float32, -0.4, 0.4)
    diagonal = jnp.stack([diag_real, diag_imag], axis=1)[..., None] * jnp.eye(NB, dtype=jnp.float32)
    return upper + diagonal


def levels(rng, extent, cuts, least, high):
    def one(dim, shards_of):
        heights = jax.random.uniform(jax.random.fold_in(jax.random.fold_in(rng, 6), dim), (shards_of,), jnp.float32, least / len(cuts), high / len(cuts))
        return jnp.repeat(jnp.exp(heights), extent[dim] // shards_of).reshape((-1,) + (1,) * (len(extent) - dim - 1))

    gain = one(*cuts[0])
    for cut in cuts[1:]:
        gain = gain * one(*cut)
    return gain


def gaussian(key, shape, deviation, reach, cuts=(), kind=jnp.bfloat16):
    result = deviation * jax.random.normal(key, shape, jnp.float32)
    if cuts:
        result = result * levels(key, shape, cuts, -0.22, 0.18)
    return jnp.clip(result, -reach, reach).astype(kind)


def setup_inputs(seed: int = 0) -> dict:
    streams_of = jax.random.split(jax.random.key(seed), 7)
    return {
        "rhs_top": gaussian(streams_of[0], (2, ABOVE, ANG), 1.0, 6.0, ((1, 32), (2, 16)), jnp.float32),
        "rhs_low": gaussian(streams_of[1], (2, 2, NB, ANG), 1.0, 6.0, ((2, 32), (3, 16)), jnp.float32),
        "inv_diag": draw_inv_diag(jax.random.fold_in(streams_of[6], 71), 0),
        "coupling": gaussian(streams_of[3], (2, NB, NB), (2 * NB) ** -0.5, 0.1875, ((1, 32),), jnp.float32),
        "panel": gaussian(streams_of[4], (2, ABOVE, 2 * NB), (4 * NB) ** -0.5, 0.125, ((1, 32), (2, 16)), jnp.float32),
        "radiation": gaussian(streams_of[5], (2, 2 * DIRS, 2 * NB), (4 * NB) ** -0.5, 0.125, ((1, 32),), jnp.float32),
    }


def complex_product(matrix, vector):
    def plain(left_side, right_side):
        return jnp.dot(left_side, right_side, precision=lax.Precision.HIGHEST, preferred_element_type=jnp.float32)
    real_part = plain(matrix[0], vector[0]) - plain(matrix[1], vector[1])
    imag_part = plain(matrix[0], vector[1]) + plain(matrix[1], vector[0])
    return jnp.stack([real_part, imag_part], axis=0)


def reference(rhs_top, rhs_low, inv_diag, coupling, panel, radiation):
    lower_part = complex_product(inv_diag[1], rhs_low[1])
    reduced = rhs_low[0] - complex_product(coupling, lower_part)
    upper_part = complex_product(inv_diag[0], reduced)
    currents = jnp.concatenate([upper_part, lower_part], axis=1)
    updated_top = rhs_top - complex_product(panel, currents)
    far_field = complex_product(radiation, currents)
    solved = jnp.stack([upper_part, lower_part], axis=0)
    return solved, updated_top, far_field
```

```python
import jax
import jax.numpy as jnp
from jax import lax
from jax.sharding import PartitionSpec as P


def product(left_side, right_side):
    return jnp.dot(left_side, right_side, precision=lax.Precision.HIGH, preferred_element_type=jnp.float32)


def rows_of(matrix):
    return matrix.reshape(matrix.shape[0] * matrix.shape[1], matrix.shape[2])


def joined(pair):
    return jnp.concatenate([pair[0], pair[1]], axis=1)


def combine(four):
    m, n = four.shape[0] // 2, four.shape[1] // 2
    real_part = four[:m, :n] - four[m:, n:]
    imag_part = four[:m, n:] + four[m:, :n]
    return jnp.concatenate([real_part, imag_part], axis=1)


def split(wide):
    n = wide.shape[1] // 2
    return jnp.stack([wide[:, :n], wide[:, n:]], axis=0)


def everyone(piece):
    count = lax.axis_size("row")
    spread = jnp.broadcast_to(piece[None], (count,) + piece.shape)
    return lax.all_to_all(spread, "row", 0, 0, tiled=True).reshape(count * piece.shape[0], piece.shape[1])


def tall_product(left_side, right_side):
    return lax.dot_general(left_side, right_side, (((0,), (0,)), ((), ())), precision=lax.Precision.HIGH, preferred_element_type=jnp.float32)


def local(rhs_top, rhs_low, inv_diag, coupling, panel, radiation):
    half = coupling.shape[2]
    wide_panel = lax.all_gather(jnp.swapaxes(panel, 1, 2), "col", axis=1, tiled=True)
    last_all = everyone(joined(rhs_low[1]))
    lower = combine(product(rows_of(inv_diag[1]), last_all))
    lower_all = everyone(lower)
    reduced = joined(rhs_low[0]) - combine(product(rows_of(coupling), lower_all))
    reduced_all = everyone(reduced)
    upper = combine(product(rows_of(inv_diag[0]), reduced_all))
    upper_all = everyone(upper)
    currents = jnp.concatenate([upper_all, lower_all], axis=0)
    far_field = split(combine(product(rows_of(radiation), currents)))
    real_rows = tall_product(wide_panel[0], currents)
    imag_rows = tall_product(wide_panel[1], currents)
    n = rhs_top.shape[2]
    updated_top = jnp.stack([
        rhs_top[0] - (real_rows[:, :n] - imag_rows[:, n:]),
        rhs_top[1] - (real_rows[:, n:] + imag_rows[:, :n]),
    ], axis=0)
    solved = jnp.stack([split(upper), split(lower)], axis=0)
    return (solved, updated_top, far_field)


def solution(mesh):
    in_specs = (
        P(None, "row", "col"),
        P(None, None, "row", "col"),
        P(None, None, "row", None),
        P(None, "row", None),
        P(None, "row", "col"),
        P(None, "row", None),
    )
    out_specs = (P(None, None, "row", "col"), P(None, "row", "col"), P(None, "row", "col"))
    return jax.shard_map(local, mesh=mesh, in_specs=in_specs, out_specs=out_specs, check_vma=False)
```

```python
import jax
import jax.numpy as jnp
from jax import lax
from jax.experimental import pallas as pl
from jax.experimental.pallas import tpu as pltpu
from jax.sharding import Mesh, PartitionSpec as P

XS, ZS = 4, 8


def product(left_side, right_side):
    return jnp.dot(left_side, right_side, precision=lax.Precision.HIGH, preferred_element_type=jnp.float32)


def exchange(pieces, axes):
    return lax.all_to_all(pieces, axes, 0, 0, tiled=True)


def everyone(piece, axis):
    count = lax.axis_size(axis)
    return exchange(jnp.broadcast_to(piece[None], (count,) + piece.shape), axis)


def complex_rows(matrix, vector):
    x, _, r, k = matrix.shape
    n = vector.shape[1]
    four = product(matrix.reshape(x * 2 * r, k), vector).reshape(x, 2, r, n)
    by_real, by_imag = four[:, 0], four[:, 1]
    turned = jnp.concatenate([-by_imag[..., n // 2:], by_imag[..., : n // 2]], axis=-1)
    return by_real + turned


def along_z(piece, before, after):
    padded = jnp.pad(piece, ((0, 0), (0, 0), (before, after)))
    got = everyone(padded, "z")
    x, r, n = padded.shape
    return jnp.swapaxes(got, 0, 1).reshape(x * ZS * r, n)


def halves(value):
    high = value.astype(jnp.bfloat16)
    return high, (value - high.astype(jnp.float32)).astype(jnp.bfloat16)


def dot_three(stacked, right_side, contract):
    m = stacked.shape[0] // 2
    high, low = halves(right_side)
    dims = (((1,), (contract,)), ((), ()))
    both = lax.dot_general(stacked, high, dims, preferred_element_type=jnp.float32)
    rest = lax.dot_general(stacked[:m], low, dims, preferred_element_type=jnp.float32)
    return both[:m] + both[m:] + rest


def parts_of(by_real, by_imag):
    n = by_real.shape[0] // 2
    return (by_real[:n] - by_imag[n:]).T, (by_real[n:] + by_imag[:n]).T


def spread(place_ref, upper_ref, lower_ref, radiation_ref, turned_ref, far_ref, solved_ref):
    s, zs, _, lanes = upper_ref.shape
    a = lanes // 4
    n = s * a
    r = solved_ref.shape[2]
    half = lower_ref.shape[1]
    x, z = place_ref[0], place_ref[1]
    right_half = x >= 2
    inner = x - 2 * right_half.astype(jnp.int32)
    upper_at = pl.multiple_of(inner * r, r)
    lower_at = pl.multiple_of((inner * zs + z) * r, r)
    mine = (
        [upper_ref[i, z, pl.ds(upper_at, r), :] for i in range(s)],
        [lower_ref[i, pl.ds(lower_at, r), :] for i in range(s)],
    )
    for block in range(2):
        pieces = [jnp.where(right_half, piece[:, 2 * a:], piece[:, :2 * a]) for piece in mine[block]]
        for part in range(2):
            solved_ref[block, part] = jnp.concatenate([piece[:, part * a:(part + 1) * a] for piece in pieces], axis=1)
    for i in range(s):
        ordered = jnp.concatenate([upper_ref[i, k, j * r:(j + 1) * r, :] for j in range(2) for k in range(zs)], axis=0)
        for block, value in enumerate((ordered, lower_ref[i])):
            high, low = halves(value.T)
            for h in range(2):
                for part in range(2):
                    at = (h * 2 + part) * a
                    to = part * n + i * a
                    k = (block * 2 + h) * half
                    turned_ref[to:to + a, k:k + half] = high[at:at + a]
                    turned_ref[2 * n + to:2 * n + to + a, k:k + half] = low[at:at + a]
    turned = turned_ref[...]
    real_part, imag_part = parts_of(dot_three(turned, radiation_ref[0], 1), dot_three(turned, radiation_ref[1], 1))
    far_ref[0] = real_part
    far_ref[1] = imag_part


def finish_kernel(place_ref, upper_ref, lower_ref, radiation_ref, panel_ref, top_ref, far_ref, solved_ref, out_ref, turned_ref):
    @pl.when(pl.program_id(0) == 0)
    def _():
        spread(place_ref, upper_ref, lower_ref, radiation_ref, turned_ref, far_ref, solved_ref)

    turned = turned_ref[...]
    real_part, imag_part = parts_of(dot_three(turned, panel_ref[0], 0), dot_three(turned, panel_ref[1], 0))
    out_ref[0] = top_ref[0] - real_part
    out_ref[1] = top_ref[1] - imag_part


def finish(place, upper, lower, radiation, wide_panel, rhs_top, r, tile=256):
    _, k, m = wide_panel.shape
    n = rhs_top.shape[2]

    def whole(shape):
        return pl.BlockSpec(shape, lambda i: (0,) * len(shape))

    far, solved = (2, radiation.shape[1], n), (2, 2, r, n)
    return pl.pallas_call(
        finish_kernel,
        out_shape=tuple(jax.ShapeDtypeStruct(shape, jnp.float32) for shape in (far, solved, rhs_top.shape)),
        grid=(m // tile,),
        in_specs=[
            pl.BlockSpec(memory_space=pltpu.SMEM),
            whole(upper.shape),
            whole(lower.shape),
            whole(radiation.shape),
            pl.BlockSpec((2, k, tile), lambda i: (0, 0, i)),
            pl.BlockSpec((2, tile, n), lambda i: (0, i, 0)),
        ],
        out_specs=(whole(far), whole(solved), pl.BlockSpec((2, tile, n), lambda i: (0, i, 0))),
        scratch_shapes=[pltpu.VMEM((4 * n, k), jnp.bfloat16)],
        compiler_params=pltpu.CompilerParams(vmem_limit_bytes=48 * 1024 * 1024),
        name="finish",
    )(place, upper, lower, radiation, wide_panel, rhs_top)


def local(rhs_top, rhs_low, inv_diag, coupling, panel, radiation):
    r, n = rhs_low.shape[2], rhs_low.shape[3]
    half = coupling.shape[2]
    a = n // XS
    matrices = lax.all_gather(jnp.stack([inv_diag[1], coupling, inv_diag[0]], axis=0), "x", axis=0)
    wide_panel = lax.all_gather(jnp.swapaxes(panel, 1, 2), "col", axis=1, tiled=True)
    quarters = jnp.stack([
        jnp.concatenate([rhs_low[block, part, :, i * a:(i + 1) * a] for block in range(2) for part in range(2)], axis=1)
        for i in range(XS)], axis=0)[:, None]
    quarters = jnp.broadcast_to(quarters, (XS, ZS, r, 4 * a)).reshape(XS * ZS, r, 4 * a)
    right = exchange(quarters, ("x", "z"))
    first = lax.dynamic_index_in_dim(right.reshape(XS, ZS, r, 4 * a), lax.axis_index("z"), 1, keepdims=False)
    first, right = lax.optimization_barrier((first, right.reshape(half, 4 * a)))
    lower_all = along_z(complex_rows(matrices[:, 0], right[:, 2 * a:]), 2 * a, 0)
    reduced = first[:, :, :2 * a] - complex_rows(matrices[:, 1], lower_all[:, 2 * a:])
    reduced_all = along_z(reduced, 0, 2 * a)
    upper = complex_rows(matrices[:, 2], reduced_all[:, :2 * a])
    upper, lower_all = lax.optimization_barrier((upper, lower_all))
    lower_pack = jnp.concatenate([lower_all[:half // 2, 2 * a:], lower_all[half // 2:, 2 * a:]], axis=1)
    upper_pack = jnp.concatenate([upper[:XS // 2], upper[XS // 2:]], axis=2).reshape(1, XS // 2 * r, 4 * a)
    upper_all = exchange(jnp.broadcast_to(upper_pack, (XS * ZS,) + upper_pack.shape[1:]), ("x", "z"))
    lower_wide = lax.all_gather(lower_pack, "x", axis=0)
    place = jnp.stack([lax.axis_index("x"), lax.axis_index("z")]).astype(jnp.int32)
    upper_all = upper_all.reshape((XS, ZS) + upper_pack.shape[1:])
    far_field, solved, updated_top = finish(place, upper_all, lower_wide, radiation, wide_panel, rhs_top, r)
    return (solved, updated_top, far_field)


def solution(mesh):
    fine = Mesh(mesh.devices.reshape(XS, ZS, -1), ("x", "z", "col"))
    row = ("x", "z")
    in_specs = (
        P(None, row, "col"),
        P(None, None, row, "col"),
        P(None, None, row, None),
        P(None, row, None),
        P(None, row, "col"),
        P(None, row, None),
    )
    out_specs = (P(None, None, row, "col"), P(None, row, "col"), P(None, row, "col"))
    return jax.shard_map(local, mesh=fine, in_specs=in_specs, out_specs=out_specs, check_vma=False)
```

```python
import jax
import jax.numpy as jnp
from jax import lax
from jax.experimental import pallas as pl
from jax.experimental.pallas import tpu as pltpu
from jax.sharding import Mesh, PartitionSpec as P

XS, ZS = 4, 8


def product(left_side, right_side):
    return jnp.dot(left_side, right_side, precision=lax.Precision.HIGH, preferred_element_type=jnp.float32)


def exchange(pieces, axes):
    return lax.all_to_all(pieces, axes, 0, 0, tiled=True)


def everyone(piece, axis):
    count = lax.axis_size(axis)
    return exchange(jnp.broadcast_to(piece[None], (count,) + piece.shape), axis)


def complex_rows(matrix, vector):
    x, _, r, k = matrix.shape
    n = vector.shape[1]
    four = product(matrix.reshape(x * 2 * r, k), vector).reshape(x, 2, r, n)
    by_real, by_imag = four[:, 0], four[:, 1]
    turned = jnp.concatenate([-by_imag[..., n // 2:], by_imag[..., : n // 2]], axis=-1)
    return by_real + turned


def along_z(piece, before, after):
    padded = jnp.pad(piece, ((0, 0), (0, 0), (before, after)))
    got = everyone(padded, "z")
    x, r, n = padded.shape
    return jnp.swapaxes(got, 0, 1).reshape(x * ZS * r, n)


def halves(value):
    high = value.astype(jnp.bfloat16)
    return high, (value - high.astype(jnp.float32)).astype(jnp.bfloat16)


def dot_three(stacked, right_side, contract):
    m = stacked.shape[0] // 2
    high, low = halves(right_side)
    dims = (((1,), (contract,)), ((), ()))
    both = lax.dot_general(stacked, high, dims, preferred_element_type=jnp.float32)
    rest = lax.dot_general(stacked[:m], low, dims, preferred_element_type=jnp.float32)
    return both[:m] + both[m:] + rest


def parts_of(by_real, by_imag):
    n = by_real.shape[0] // 2
    return (by_real[:n] - by_imag[n:]).T, (by_real[n:] + by_imag[:n]).T


def spread(place_ref, upper_ref, lower_ref, radiation_ref, turned_ref, far_ref, solved_ref):
    s, zs, _, lanes = upper_ref.shape
    a = lanes // 4
    n = s * a
    r = solved_ref.shape[2]
    half = lower_ref.shape[1]
    x, z = place_ref[0], place_ref[1]
    right_half = x >= 2
    inner = x - 2 * right_half.astype(jnp.int32)
    upper_at = pl.multiple_of(inner * r, r)
    lower_at = pl.multiple_of((inner * zs + z) * r, r)
    mine = (
        [upper_ref[i, z, pl.ds(upper_at, r), :] for i in range(s)],
        [lower_ref[i, pl.ds(lower_at, r), :] for i in range(s)],
    )
    for block in range(2):
        pieces = [jnp.where(right_half, piece[:, 2 * a:], piece[:, :2 * a]) for piece in mine[block]]
        for part in range(2):
            solved_ref[block, part] = jnp.concatenate([piece[:, part * a:(part + 1) * a] for piece in pieces], axis=1)
    for i in range(s):
        ordered = jnp.concatenate([upper_ref[i, k, j * r:(j + 1) * r, :] for j in range(2) for k in range(zs)], axis=0)
        for block, value in enumerate((ordered, lower_ref[i])):
            high, low = halves(value.T)
            for h in range(2):
                for part in range(2):
                    at = (h * 2 + part) * a
                    to = part * n + i * a
                    k = (block * 2 + h) * half
                    turned_ref[to:to + a, k:k + half] = high[at:at + a]
                    turned_ref[2 * n + to:2 * n + to + a, k:k + half] = low[at:at + a]
    turned = turned_ref[...]
    real_part, imag_part = parts_of(dot_three(turned, radiation_ref[0], 1), dot_three(turned, radiation_ref[1], 1))
    far_ref[0] = real_part
    far_ref[1] = imag_part


def finish_kernel(place_ref, upper_ref, lower_ref, radiation_ref, panel_ref, top_ref, far_ref, solved_ref, out_ref, turned_ref):
    @pl.when(pl.program_id(0) == 0)
    def _():
        spread(place_ref, upper_ref, lower_ref, radiation_ref, turned_ref, far_ref, solved_ref)

    turned = turned_ref[...]
    real_part, imag_part = parts_of(dot_three(turned, panel_ref[0], 0), dot_three(turned, panel_ref[1], 0))
    out_ref[0] = top_ref[0] - real_part
    out_ref[1] = top_ref[1] - imag_part


def finish(place, upper, lower, radiation, wide_panel, rhs_top, r, tile=512):
    _, k, m = wide_panel.shape
    n = rhs_top.shape[2]

    def whole(shape):
        return pl.BlockSpec(shape, lambda i: (0,) * len(shape))

    far, solved = (2, radiation.shape[1], n), (2, 2, r, n)
    return pl.pallas_call(
        finish_kernel,
        out_shape=tuple(jax.ShapeDtypeStruct(shape, jnp.float32) for shape in (far, solved, rhs_top.shape)),
        grid=(m // tile,),
        in_specs=[
            pl.BlockSpec(memory_space=pltpu.SMEM),
            whole(upper.shape),
            whole(lower.shape),
            whole(radiation.shape),
            pl.BlockSpec((2, k, tile), lambda i: (0, 0, i)),
            pl.BlockSpec((2, tile, n), lambda i: (0, i, 0)),
        ],
        out_specs=(whole(far), whole(solved), pl.BlockSpec((2, tile, n), lambda i: (0, i, 0))),
        scratch_shapes=[pltpu.VMEM((4 * n, k), jnp.bfloat16)],
        compiler_params=pltpu.CompilerParams(vmem_limit_bytes=48 * 1024 * 1024),
        name="finish",
    )(place, upper, lower, radiation, wide_panel, rhs_top)


def local(rhs_top, rhs_low, inv_diag, coupling, panel, radiation):
    r, n = rhs_low.shape[2], rhs_low.shape[3]
    half = coupling.shape[2]
    a = n // XS
    matrices = lax.all_gather(jnp.concatenate([inv_diag, coupling[None]], axis=0), "x", axis=0)
    wide_panel = lax.all_gather(jnp.swapaxes(panel, 1, 2), "col", axis=1, tiled=True)
    quarters = jnp.stack([
        jnp.concatenate([rhs_low[block, part, :, i * a:(i + 1) * a] for block in range(2) for part in range(2)], axis=1)
        for i in range(XS)], axis=0)[:, None]
    quarters = jnp.broadcast_to(quarters, (XS, ZS, r, 4 * a)).reshape(XS * ZS, r, 4 * a)
    right = exchange(quarters, ("x", "z"))
    first = lax.dynamic_index_in_dim(right.reshape(XS, ZS, r, 4 * a), lax.axis_index("z"), 1, keepdims=False)
    first, right = lax.optimization_barrier((first, right.reshape(half, 4 * a)))
    lower_all = along_z(complex_rows(matrices[:, 1], right[:, 2 * a:]), 2 * a, 0)
    reduced = first[:, :, :2 * a] - complex_rows(matrices[:, 2], lower_all[:, 2 * a:])
    reduced_all = along_z(reduced, 0, 2 * a)
    upper = complex_rows(matrices[:, 0], reduced_all[:, :2 * a])
    upper, lower_all = lax.optimization_barrier((upper, lower_all))
    lower_pack = jnp.concatenate([lower_all[:half // 2, 2 * a:], lower_all[half // 2:, 2 * a:]], axis=1)
    upper_pack = jnp.concatenate([upper[:XS // 2], upper[XS // 2:]], axis=2).reshape(1, XS // 2 * r, 4 * a)
    upper_all = exchange(jnp.broadcast_to(upper_pack, (XS * ZS,) + upper_pack.shape[1:]), ("x", "z"))
    lower_wide = lax.all_gather(lower_pack, "x", axis=0)
    place = jnp.stack([lax.axis_index("x"), lax.axis_index("z")]).astype(jnp.int32)
    upper_all = upper_all.reshape((XS, ZS) + upper_pack.shape[1:])
    far_field, solved, updated_top = finish(place, upper_all, lower_wide, radiation, wide_panel, rhs_top, r)
    return (solved, updated_top, far_field)


def solution(mesh):
    fine = Mesh(mesh.devices.reshape(XS, ZS, -1), ("x", "z", "col"))
    row = ("x", "z")
    in_specs = (
        P(None, row, "col"),
        P(None, None, row, "col"),
        P(None, None, row, None),
        P(None, row, None),
        P(None, row, "col"),
        P(None, row, None),
    )
    out_specs = (P(None, None, row, "col"), P(None, row, "col"), P(None, row, "col"))
    return jax.shard_map(local, mesh=fine, in_specs=in_specs, out_specs=out_specs, check_vma=False)
```

```python
import jax
import jax.numpy as jnp
from jax import lax
from jax.experimental import pallas as pl
from jax.experimental.pallas import tpu as pltpu
from jax.sharding import Mesh, PartitionSpec as P

XS, ZS = 4, 8


def product(left_side, right_side):
    return jnp.dot(left_side, right_side, precision=lax.Precision.HIGH, preferred_element_type=jnp.float32)


def exchange(pieces, axes):
    return lax.all_to_all(pieces, axes, 0, 0, tiled=True)


def everyone(piece, axis):
    count = lax.axis_size(axis)
    return exchange(jnp.broadcast_to(piece[None], (count,) + piece.shape), axis)


def complex_rows(matrix, vector):
    x, _, r, k = matrix.shape
    n = vector.shape[1]
    four = product(matrix.reshape(x * 2 * r, k), vector).reshape(x, 2, r, n)
    by_real, by_imag = four[:, 0], four[:, 1]
    turned = jnp.concatenate([-by_imag[..., n // 2:], by_imag[..., : n // 2]], axis=-1)
    return by_real + turned


def along_z(piece, before, after):
    padded = jnp.pad(piece, ((0, 0), (0, 0), (before, after)))
    got = everyone(padded, "z")
    x, r, n = padded.shape
    return jnp.swapaxes(got, 0, 1).reshape(x * ZS * r, n)


def halves(value):
    high = value.astype(jnp.bfloat16)
    return high, (value - high.astype(jnp.float32)).astype(jnp.bfloat16)


def dot_three(stacked, right_side, contract):
    m = stacked.shape[0] // 2
    high, low = halves(right_side)
    dims = (((1,), (contract,)), ((), ()))
    both = lax.dot_general(stacked, high, dims, preferred_element_type=jnp.float32)
    rest = lax.dot_general(stacked[:m], low, dims, preferred_element_type=jnp.float32)
    return both[:m] + both[m:] + rest


def parts_of(by_real, by_imag):
    n = by_real.shape[0] // 2
    return (by_real[:n] - by_imag[n:]).T, (by_real[n:] + by_imag[:n]).T


def spread(place_ref, upper_ref, lower_ref, radiation_ref, turned_ref, far_ref, solved_ref):
    s, zs, _, lanes = upper_ref.shape
    a = lanes // 4
    n = s * a
    r = solved_ref.shape[2]
    half = lower_ref.shape[1]
    x, z = place_ref[0], place_ref[1]
    right_half = x >= 2
    inner = x - 2 * right_half.astype(jnp.int32)
    upper_at = pl.multiple_of(inner * r, r)
    lower_at = pl.multiple_of((inner * zs + z) * r, r)
    mine = (
        [upper_ref[i, z, pl.ds(upper_at, r), :] for i in range(s)],
        [lower_ref[i, pl.ds(lower_at, r), :] for i in range(s)],
    )
    for block in range(2):
        pieces = [jnp.where(right_half, piece[:, 2 * a:], piece[:, :2 * a]) for piece in mine[block]]
        for part in range(2):
            solved_ref[block, part] = jnp.concatenate([piece[:, part * a:(part + 1) * a] for piece in pieces], axis=1)
    for i in range(s):
        ordered = jnp.concatenate([upper_ref[i, k, j * r:(j + 1) * r, :] for j in range(2) for k in range(zs)], axis=0)
        for block, value in enumerate((ordered, lower_ref[i])):
            high, low = halves(value.T)
            for h in range(2):
                for part in range(2):
                    at = (h * 2 + part) * a
                    to = part * n + i * a
                    k = (block * 2 + h) * half
                    turned_ref[to:to + a, k:k + half] = high[at:at + a]
                    turned_ref[2 * n + to:2 * n + to + a, k:k + half] = low[at:at + a]
    turned = turned_ref[...]
    real_part, imag_part = parts_of(dot_three(turned, radiation_ref[0], 1), dot_three(turned, radiation_ref[1], 1))
    far_ref[0] = real_part
    far_ref[1] = imag_part


def finish_kernel(place_ref, upper_ref, lower_ref, radiation_ref, panel_ref, top_ref, far_ref, solved_ref, out_ref, turned_ref, tiles_ref, arrived):
    count, _, _, tile = tiles_ref.shape
    copies = [
        pltpu.make_async_copy(panel_ref.at[:, :, i * tile:(i + 1) * tile], tiles_ref.at[i], arrived.at[i])
        for i in range(count)
    ]
    for copy in copies:
        copy.start()
    spread(place_ref, upper_ref, lower_ref, radiation_ref, turned_ref, far_ref, solved_ref)
    turned = turned_ref[...]
    for i, copy in enumerate(copies):
        copy.wait()
        real_part, imag_part = parts_of(dot_three(turned, tiles_ref[i, 0], 0), dot_three(turned, tiles_ref[i, 1], 0))
        rows = slice(i * tile, (i + 1) * tile)
        out_ref[0, rows] = top_ref[0, rows] - real_part
        out_ref[1, rows] = top_ref[1, rows] - imag_part


def finish(place, upper, lower, radiation, wide_panel, rhs_top, r, tile=512):
    _, k, m = wide_panel.shape
    n = rhs_top.shape[2]
    whole = pl.BlockSpec(memory_space=pltpu.VMEM)
    far, solved = (2, radiation.shape[1], n), (2, 2, r, n)
    return pl.pallas_call(
        finish_kernel,
        out_shape=tuple(jax.ShapeDtypeStruct(shape, jnp.float32) for shape in (far, solved, rhs_top.shape)),
        in_specs=[pl.BlockSpec(memory_space=pltpu.SMEM), whole, whole, whole, pl.BlockSpec(memory_space=pl.ANY), whole],
        out_specs=(whole, whole, whole),
        scratch_shapes=[
            pltpu.VMEM((4 * n, k), jnp.bfloat16),
            pltpu.VMEM((m // tile, 2, k, tile), jnp.float32),
            pltpu.SemaphoreType.DMA((m // tile,)),
        ],
        compiler_params=pltpu.CompilerParams(vmem_limit_bytes=48 * 1024 * 1024),
        name="finish",
    )(place, upper, lower, radiation, wide_panel, rhs_top)


def local(rhs_top, rhs_low, inv_diag, coupling, panel, radiation):
    r, n = rhs_low.shape[2], rhs_low.shape[3]
    half = coupling.shape[2]
    a = n // XS
    matrices = lax.all_gather(jnp.concatenate([inv_diag, coupling[None]], axis=0), "x", axis=0)
    wide_panel = lax.all_gather(jnp.swapaxes(panel, 1, 2), "col", axis=1, tiled=True)
    quarters = jnp.stack([
        jnp.concatenate([rhs_low[block, part, :, i * a:(i + 1) * a] for block in range(2) for part in range(2)], axis=1)
        for i in range(XS)], axis=0)[:, None]
    quarters = jnp.broadcast_to(quarters, (XS, ZS, r, 4 * a)).reshape(XS * ZS, r, 4 * a)
    right = exchange(quarters, ("x", "z"))
    first = lax.dynamic_index_in_dim(right.reshape(XS, ZS, r, 4 * a), lax.axis_index("z"), 1, keepdims=False)
    first, right = lax.optimization_barrier((first, right.reshape(half, 4 * a)))
    lower_all = along_z(complex_rows(matrices[:, 1], right[:, 2 * a:]), 2 * a, 0)
    reduced = first[:, :, :2 * a] - complex_rows(matrices[:, 2], lower_all[:, 2 * a:])
    reduced_all = along_z(reduced, 0, 2 * a)
    upper = complex_rows(matrices[:, 0], reduced_all[:, :2 * a])
    upper, lower_all = lax.optimization_barrier((upper, lower_all))
    lower_pack = jnp.concatenate([lower_all[:half // 2, 2 * a:], lower_all[half // 2:, 2 * a:]], axis=1)
    upper_pack = jnp.concatenate([upper[:XS // 2], upper[XS // 2:]], axis=2).reshape(1, XS // 2 * r, 4 * a)
    upper_all = exchange(jnp.broadcast_to(upper_pack, (XS * ZS,) + upper_pack.shape[1:]), ("x", "z"))
    lower_wide = lax.all_gather(lower_pack, "x", axis=0)
    place = jnp.stack([lax.axis_index("x"), lax.axis_index("z")]).astype(jnp.int32)
    upper_all = upper_all.reshape((XS, ZS) + upper_pack.shape[1:])
    far_field, solved, updated_top = finish(place, upper_all, lower_wide, radiation, wide_panel, rhs_top, r)
    return (solved, updated_top, far_field)


def solution(mesh):
    fine = Mesh(mesh.devices.reshape(XS, ZS, -1), ("x", "z", "col"))
    row = ("x", "z")
    in_specs = (
        P(None, row, "col"),
        P(None, None, row, "col"),
        P(None, None, row, None),
        P(None, row, None),
        P(None, row, "col"),
        P(None, row, None),
    )
    out_specs = (P(None, None, row, "col"), P(None, row, "col"), P(None, row, "col"))
    return jax.shard_map(local, mesh=fine, in_specs=in_specs, out_specs=out_specs, check_vma=False)
```
